32 devices in a mesh: req: 8 (over y, x, core), mp: 4 (over z).
Axes of the slice: x: 2, y: 2, z: 4, core: 2. Of those that a mesh axis runs over, the one named last changes fastest.
Arguments:
- latents: bfloat16 [16, 1, 384, 416], P('req', None, 'mp'), may hold values from -12 to 12
- prior_frame_cache: bfloat16 [16, 2, 384, 416], P('req', None, 'mp'), may hold values from -6 to 6
- move_to: int32 [16], P('req'), may hold values from 0 to 15, as said below
- counts: int32 [8], P('req'), may hold values from 1 to 2, as said below
- norm_gain: bfloat16 [384], P('mp'), may hold values from 0.5 to 1.5
- conv_weight: bfloat16 [27, 384, 384], P(None, 'mp'), may hold values from -0.0625 to 0.0625
- conv_bias: float32 [384], P('mp'), may hold values from -1.5 to 1.5
Outputs:
- decoded: bfloat16 [16, 1, 384, 416], P('req', None, 'mp')
- new_cache: bfloat16 [16, 2, 384, 416], P('req', None, 'mp')
The draws below stay inside these ranges and needn't reach their ends.
Inputs may be any that keep to these rules, and one draw needn't show every extreme that they name: move_to is a permutation of the slots; a stream's new slot lies on its old index of req or on the next or previous one, the last and first index being neighbours; every index hands exactly 1 stream to each neighbour and takes the same number back from it. `counts`: some index of req is full and some other holds a single stream.
All inputs are finite; a program needn't handle non-finite values.
Results may differ from the reference program's by a relative error of at most 0.0018.
Values may be sent and summed in bfloat16 or wider, within the bound.
A program may use at most 64 MiB of HBM per device.

```python
import math
import jax
import jax.numpy as jnp
from jax import lax

SECTION_CHANNELS = 384
SLOTS_PER_INDEX = 2
LATENT_ROWS = 4
LATENT_COLUMNS = 104
LATENT_FRAMES = 1
CAP = 1
STREAM_SLOTS = 16
FRAME_PIXELS = 416


def draw_latents(key, part):
    base_key = jax.random.fold_in(key, 101)
    key_values = jax.random.fold_in(base_key, 0)
    array_shape = (STREAM_SLOTS, LATENT_FRAMES, SECTION_CHANNELS, LATENT_ROWS * LATENT_COLUMNS)
    rising = 0.6 * jnp.exp(math.log(3.0) * jnp.arange(SECTION_CHANNELS, dtype=jnp.float32) / (SECTION_CHANNELS - 1))
    values = jnp.clip(jax.random.normal(key_values, array_shape, jnp.float32), -4.0, 4.0)
    return jnp.clip(values * rising[:, None], -12.0, 12.0).astype(jnp.bfloat16)


def draw_move_to(key, part):
    base_key = jax.random.fold_in(key, 202)
    key_order = jax.random.fold_in(base_key, 7)
    member_slots = STREAM_SLOTS // SLOTS_PER_INDEX
    flows = jnp.full((member_slots,), CAP, jnp.int32)
    scores = jax.random.randint(key_order, (member_slots, SLOTS_PER_INDEX), 0, 1 << 20) * SLOTS_PER_INDEX + jnp.arange(SLOTS_PER_INDEX)[None, :]
    shuffle = jnp.argsort(scores, axis=1).astype(jnp.int32)
    ranking = jnp.argsort(shuffle, axis=1).astype(jnp.int32)
    rows_here = jnp.arange(member_slots, dtype=jnp.int32)
    right_dev = (rows_here + 1) % member_slots
    left_dev = (rows_here - 1) % member_slots
    flows_left = flows[left_dev]
    index_right = jnp.clip(SLOTS_PER_INDEX - flows[:, None] + ranking, 0, SLOTS_PER_INDEX - 1)
    slot_right = jnp.take_along_axis(shuffle[right_dev], index_right, axis=1)
    index_left = jnp.clip(ranking - (SLOTS_PER_INDEX - flows_left[:, None]), 0, SLOTS_PER_INDEX - 1)
    slot_left = jnp.take_along_axis(shuffle[left_dev], index_left, axis=1)
    goes_right = ranking < flows[:, None]
    goes_left = ranking >= SLOTS_PER_INDEX - flows_left[:, None]
    stays_slot = rows_here[:, None] * SLOTS_PER_INDEX + jnp.arange(SLOTS_PER_INDEX, dtype=jnp.int32)[None, :]
    block_output = jnp.where(goes_right, right_dev[:, None] * SLOTS_PER_INDEX + slot_right, jnp.where(goes_left, left_dev[:, None] * SLOTS_PER_INDEX + slot_left, stays_slot))
    return block_output.reshape(STREAM_SLOTS).astype(jnp.int32)


def draw_counts(key, part):
    base_key = jax.random.fold_in(key, 303)
    key_load, key_full, key_single = jax.random.split(base_key, 3)
    member_slots = STREAM_SLOTS // SLOTS_PER_INDEX
    loads = jax.random.randint(key_load, (member_slots,), 1, SLOTS_PER_INDEX + 1)
    full_at = jax.random.randint(key_full, (), 0, member_slots)
    single_at = (full_at + jax.random.randint(key_single, (), 1, member_slots)) % member_slots
    rows_here = jnp.arange(member_slots)
    loads = jnp.where(rows_here == single_at, 1, loads)
    return jnp.where(rows_here == full_at, SLOTS_PER_INDEX, loads).astype(jnp.int32)


def block_levels(stream_key, dims, shards, least, largest):
    def one(dim, parts):
        steps = jax.random.uniform(jax.random.fold_in(jax.random.fold_in(stream_key, 6), dim), (parts,), jnp.float32, least / len(shards), largest / len(shards))
        return jnp.repeat(jnp.exp(steps), dims[dim] // parts).reshape((-1,) + (1,) * (len(dims) - dim - 1))

    gain = one(*shards[0])
    for cut in shards[1:]:
        gain = gain * one(*cut)
    return gain


def noise(key, shape, width, most, shards=(), kind=jnp.bfloat16):
    values = jax.random.normal(key, shape, jnp.float32) * width
    if len(shards) > 0:
        values = block_levels(key, shape, shards, -0.22, 0.18) * values
    return jnp.clip(values, min=-most, max=most).astype(kind)


def setup_inputs(seed: int = 0) -> dict:
    arg_keys = jax.random.split(jax.random.key(seed), 8)
    latents = draw_latents(jax.random.fold_in(arg_keys[7], 71), 0)
    prior_frame_cache = noise(arg_keys[1], (STREAM_SLOTS, 2, SECTION_CHANNELS, FRAME_PIXELS), 1.0, 6.0, ((0, 8), (2, 4)))
    move_to = draw_move_to(jax.random.fold_in(arg_keys[7], 71), 0)
    counts = draw_counts(jax.random.fold_in(arg_keys[7], 71), 0)
    norm_gain = jnp.clip(0.5 + 1.0 * jax.random.uniform(arg_keys[4], (SECTION_CHANNELS,), jnp.float32) ** block_levels(arg_keys[4], (SECTION_CHANNELS,), ((0, 4),), -0.2, 0.2), 0.5, 1.5).astype(jnp.bfloat16)
    conv_weight = noise(arg_keys[5], (27, SECTION_CHANNELS, SECTION_CHANNELS), (27 * SECTION_CHANNELS) ** -0.5, 0.0625, ((1, 4),))
    conv_bias = noise(arg_keys[6], (SECTION_CHANNELS,), 0.3, 1.5, ((0, 4),), jnp.float32)
    return dict(latents=latents, prior_frame_cache=prior_frame_cache, move_to=move_to, counts=counts, norm_gain=norm_gain, conv_weight=conv_weight, conv_bias=conv_bias)


def apply_taps(running, shard_in, weights, row_width):
    frames = shard_in.shape[1] - 2
    pixels = shard_in.shape[3]
    padded = jnp.pad(shard_in, ((0, 0), (0, 0), (0, 0), (row_width + 1, row_width + 1)))
    column = jnp.arange(pixels + 2 * row_width) % row_width
    for step_x in range(3):
        inside = ((column + step_x - 1 >= 0) & (column + step_x - 1 < row_width)).astype(shard_in.dtype)
        shifted = padded[:, :, :, step_x:step_x + pixels + 2 * row_width] * inside
        for step_y in range(3):
            window = shifted[:, :, :, step_y * row_width:step_y * row_width + pixels]
            for step_t in range(3):
                tap_weight = weights[step_t * 9 + step_y * 3 + step_x].astype(jnp.float32)
                running = running + jnp.einsum('oc,stcp->stop', tap_weight, window[:, step_t:step_t + frames].astype(jnp.float32))
    return running

def reference(latents, prior_frame_cache, move_to, counts, norm_gain, conv_weight, conv_bias):
    slot_total = latents.shape[0]
    per_device = slot_total // counts.shape[0]
    moved = jnp.zeros_like(prior_frame_cache).at[move_to].set(prior_frame_cache)
    slot_ids = jnp.arange(slot_total, dtype=jnp.int32)
    live = slot_ids % per_device < jnp.repeat(counts, per_device)
    live = live[:, None, None, None]
    values = latents.astype(jnp.float32)
    squares = lax.optimization_barrier(jnp.sum(values * values, axis=2, keepdims=True))
    normed = values * lax.rsqrt(squares / SECTION_CHANNELS + 1e-06) * norm_gain.astype(jnp.float32)[:, None]
    hidden = jax.nn.silu(normed).astype(jnp.bfloat16)
    extended = jnp.concatenate([moved, hidden], axis=1)

    def single_slot(slot_data):
        start_zero = jnp.zeros((1, LATENT_FRAMES, SECTION_CHANNELS, slot_data.shape[2]), jnp.float32)
        return apply_taps(start_zero, slot_data[None], conv_weight, LATENT_COLUMNS)[0]
    conv_sum = lax.map(single_slot, extended) + conv_bias.astype(jnp.float32)[:, None]
    decoded = jnp.where(live, values + conv_sum, jnp.zeros_like(conv_sum)).astype(jnp.bfloat16)
    new_cache = extended[:, LATENT_FRAMES:]
    return (decoded, new_cache)
```

```python
import functools

import jax
import jax.numpy as jnp
from jax import lax
from jax.experimental import pallas as pl
from jax.experimental.pallas import tpu as pltpu
from jax.sharding import PartitionSpec as P

SECTION_CHANNELS = 384
LATENT_COLUMNS = 104


def shifted_2(block, axis, distance):
    devices = range(lax.axis_size(axis))
    route = [((i - distance) % len(devices), i) for i in devices]
    return lax.ppermute(block, axis, route)


def apply_taps(running, shard_in, weights, row_width):
    frames = shard_in.shape[1] - 2
    pixels = shard_in.shape[3]
    padded = jnp.pad(shard_in, ((0, 0), (0, 0), (0, 0), (row_width + 1, row_width + 1)))
    column = jnp.arange(pixels + 2 * row_width) % row_width
    for step_x in range(3):
        inside = ((column + step_x - 1 >= 0) & (column + step_x - 1 < row_width)).astype(
            shard_in.dtype
        )
        shifted = padded[:, :, :, step_x : step_x + pixels + 2 * row_width] * inside
        for step_y in range(3):
            window = shifted[:, :, :, step_y * row_width : step_y * row_width + pixels]
            for step_t in range(3):
                running = running + jnp.einsum(
                    "oc,stcp->stop",
                    weights[step_t * 9 + step_y * 3 + step_x],
                    window[:, step_t : step_t + frames],
                    preferred_element_type=jnp.float32,
                )
    return running


def pack_slots(prior_frame_cache, chosen, target, capacity):
    ranking = jnp.cumsum(chosen.astype(jnp.int32)) - 1
    picker = (chosen[None, :] & (ranking[None, :] == jnp.arange(capacity)[:, None])).astype(
        jnp.bfloat16
    )
    blocks = jnp.einsum(
        "cs,sfkp->cfkp", picker, prior_frame_cache, preferred_element_type=jnp.float32
    ).astype(jnp.bfloat16)
    labels = (jnp.dot(picker.astype(jnp.float32), (target + 1).astype(jnp.float32)) - 1.0).astype(
        jnp.bfloat16
    )
    return (blocks, labels)


def migrate(prior_frame_cache, move_to):
    slot_count = prior_frame_cache.shape[0]
    member_slots = lax.axis_size("req")
    position = lax.axis_index("req")
    capacity = slot_count // 2
    device = move_to // slot_count
    target = move_to % slot_count
    offset = (device - position) % member_slots
    goes_right = offset == 1
    goes_left = offset == member_slots - 1
    stays_put = offset == 0
    blocks_right, labels_right = pack_slots(prior_frame_cache, goes_right, target, capacity)
    blocks_left, labels_left = pack_slots(prior_frame_cache, goes_left, target, capacity)
    from_left = shifted_2((blocks_right, labels_right), "req", 1)
    from_right = shifted_2((blocks_left, labels_left), "req", -1)
    sources = jnp.concatenate([prior_frame_cache, from_left[0], from_right[0]], axis=0)
    own_labels = jnp.where(stays_put, target, -1).astype(jnp.float32)
    labels = jnp.concatenate(
        [own_labels, from_left[1].astype(jnp.float32), from_right[1].astype(jnp.float32)]
    )
    placing = (labels[None, :] == jnp.arange(slot_count, dtype=jnp.float32)[:, None]).astype(
        jnp.bfloat16
    )
    return jnp.einsum("ns,sfkp->nfkp", placing, sources, preferred_element_type=jnp.float32).astype(
        jnp.bfloat16
    )


def normalize(values, squares, gains):
    scaled = (
        values.astype(jnp.float32)
        * lax.rsqrt(squares / SECTION_CHANNELS + 1e-06)
        * gains.astype(jnp.float32)[:, None]
    )
    return jax.nn.silu(scaled).astype(jnp.bfloat16)


def shards_plain(latents, prior_frame_cache, move_to, counts, norm_gain, conv_weight, conv_bias):
    moved = migrate(prior_frame_cache, move_to)
    slot_count = latents.shape[0]
    frames = latents.shape[1]
    live = (jnp.arange(slot_count) < counts[0])[:, None, None, None]
    start_zero = jnp.zeros(
        (slot_count, frames, conv_weight.shape[1], latents.shape[3]), jnp.float32
    )
    values = latents.astype(jnp.float32)
    partial_squares = jnp.sum(values * values, axis=2, keepdims=True)
    squares = lax.psum(partial_squares, "mp")
    hidden = normalize(latents, squares, norm_gain)
    extended = jnp.concatenate([moved, hidden], axis=1)
    conv_sum = apply_taps(
        start_zero, lax.all_gather(extended, "mp", axis=2, tiled=True), conv_weight, LATENT_COLUMNS
    )
    total = latents.astype(jnp.float32) + conv_sum + conv_bias[:, None]
    decoded = jnp.where(live, total, jnp.zeros_like(total)).astype(jnp.bfloat16)
    new_cache = extended[:, frames:]
    return (decoded, new_cache)


MESH = pl.DeviceIdType.MESH


def lane_pad(n):
    return (n + 127) // 128 * 128


def column_of(row):
    n = row.shape[1]
    square = lax.broadcasted_iota(jnp.int32, (n, n), 0) == lax.broadcasted_iota(
        jnp.int32, (n, n), 1
    )
    return jnp.sum(jnp.where(square, jnp.broadcast_to(row, (n, n)), 0.0), axis=1, keepdims=True)


def pack_pair(first, second, extra, packed):
    rows, pixels = first.shape
    tail = jnp.broadcast_to(extra, (rows, packed - 2 * pixels))
    return jnp.concatenate([first, second, tail], axis=1)


def second_half(pair, pixels, wide):
    start = pixels // 128 * 128
    part = pair[:, start : start + wide].astype(jnp.float32)
    return pltpu.roll(part, wide - pixels % 128, axis=1).astype(jnp.bfloat16)


def block_kernel(
    n,
    ring,
    row_width,
    move_ref,
    counts_ref,
    lat_ref,
    cache_ref,
    gain_ref,
    bias_ref,
    w_ref,
    dec_ref,
    new_ref,
    wcat,
    gath,
    mig_out,
    mig_in,
    stack,
    acc,
    w_sem,
    mig_send,
    mig_recv,
    up_send,
    down_send,
    ag_recv,
):
    me = lax.axis_index("mp")
    pos = lax.axis_index("req")
    rows, pixels = lat_ref.shape[2], lat_ref.shape[3]
    packed = gath.shape[3]
    wide = stack.shape[2]
    channels = n * rows
    right, left = lax.rem(pos + 1, ring), lax.rem(pos + ring - 1, ring)

    w_copies = []
    for kt in range(3):
        copy = pltpu.make_async_copy(
            w_ref.at[pl.ds(9 * kt, 9)],
            wcat.at[:, :, pl.ds(channels * kt, channels)],
            w_sem.at[kt],
        )
        copy.start()
        w_copies.append(copy)

    barrier = pltpu.get_barrier_semaphore()
    for neighbour in (right, left):
        pl.semaphore_signal(barrier, inc=1, device_id={"req": neighbour}, device_id_type=MESH)

    @pl.when(me < n - 1)
    def _():
        pl.semaphore_signal(barrier, inc=1, device_id={"mp": me + 1}, device_id_type=MESH)

    @pl.when(me > 0)
    def _():
        pl.semaphore_signal(barrier, inc=1, device_id={"mp": me - 1}, device_id_type=MESH)

    gain = column_of(gain_ref[...].astype(jnp.float32))
    gath[0, me] = pack_pair(
        lat_ref[0, 0].astype(jnp.float32), lat_ref[1, 0].astype(jnp.float32), gain, packed
    ).astype(jnp.bfloat16)

    inner = (me > 0) & (me < n - 1)

    @pl.when(inner)
    def _():
        pl.semaphore_wait(barrier, 4)

    @pl.when(jnp.logical_not(inner))
    def _():
        pl.semaphore_wait(barrier, 3)

    def up_copy(j, src):
        return pltpu.make_async_remote_copy(
            src_ref=gath.at[j, src],
            dst_ref=gath.at[j, src],
            send_sem=up_send.at[j, src],
            recv_sem=ag_recv.at[j, src],
            device_id={"mp": me + 1},
            device_id_type=MESH,
        )

    def down_copy(j, src):
        return pltpu.make_async_remote_copy(
            src_ref=gath.at[j, src],
            dst_ref=gath.at[j, src],
            send_sem=down_send.at[j, src],
            recv_sem=ag_recv.at[j, src],
            device_id={"mp": me - 1},
            device_id_type=MESH,
        )

    def send_own(j):
        @pl.when(me < n - 1)
        def _():
            up_copy(j, me).start()

        @pl.when(me > 0)
        def _():
            down_copy(j, me).start()

    def relay(j, d):
        @pl.when(me - d >= 0)
        def _():
            down_copy(j, me - d).wait_recv()

            @pl.when(me < n - 1)
            def _():
                up_copy(j, me - d).start()

        @pl.when(me + d <= n - 1)
        def _():
            up_copy(j, me + d).wait_recv()

            @pl.when(me > 0)
            def _():
                down_copy(j, me + d).start()

    send_own(0)

    slots = lat_ref.shape[0]
    offset = lax.rem(lax.div(move_ref[0], slots) - pos + ring, ring)
    first_right = jnp.where(offset == 1, 1.0, 0.0).astype(jnp.float32)
    pairs = []
    for s in range(2):
        label = jnp.full((rows, 1), lax.rem(move_ref[s], slots), jnp.int32).astype(jnp.float32)
        pairs.append(
            pack_pair(
                cache_ref[s, 0].astype(jnp.float32),
                cache_ref[s, 1].astype(jnp.float32),
                label,
                packed,
            )
        )
    pick = jnp.full((rows, packed), first_right, jnp.float32) > 0.5
    mig_out[0] = jnp.where(pick, pairs[0], pairs[1]).astype(jnp.bfloat16)
    mig_out[1] = jnp.where(pick, pairs[1], pairs[0]).astype(jnp.bfloat16)
    moves = []
    for k, neighbour in enumerate((right, left)):
        copy = pltpu.make_async_remote_copy(
            src_ref=mig_out.at[k],
            dst_ref=mig_in.at[k],
            send_sem=mig_send.at[k],
            recv_sem=mig_recv.at[k],
            device_id={"req": neighbour},
            device_id_type=MESH,
        )
        copy.start()
        moves.append(copy)

    relay(0, 1)
    for copy in moves:
        copy.wait_recv()
    from_left = mig_in[0].astype(jnp.float32)
    from_right = mig_in[1].astype(jnp.float32)
    to_second = jnp.broadcast_to(from_left[:, 2 * pixels : 2 * pixels + 1], (rows, packed)) > 0.5
    gath[1, me] = jnp.where(to_second, from_right, from_left).astype(jnp.bfloat16)
    gath[2, me] = jnp.where(to_second, from_left, from_right).astype(jnp.bfloat16)
    send_own(1)
    send_own(2)
    for d in range(2, n):
        relay(0, d)

    own = pl.multiple_of(me * rows, rows)
    values = gath[0].reshape(channels, packed).astype(jnp.float32)
    gains = values[:, 2 * pixels : 2 * pixels + 1]
    squares = jnp.sum(values * values, axis=0, keepdims=True)
    scaled = values * lax.rsqrt(squares / channels + 1e-06) * gains
    hidden = (scaled / (1.0 + jnp.exp(-scaled))).astype(jnp.bfloat16)
    stack[0, pl.ds(2 * channels, channels)] = hidden[:, :wide]
    stack[1, pl.ds(2 * channels, channels)] = second_half(hidden, pixels, wide)
    for copy in w_copies:
        copy.wait()
    taps = 9 * rows
    for s in range(2):
        new_ref[s, 1] = stack[s, pl.ds(2 * channels + own, rows), :pixels]
        acc[s] = jnp.dot(
            wcat[:, :, 2 * channels :].reshape(taps, channels),
            stack[s, pl.ds(2 * channels, channels)],
            preferred_element_type=jnp.float32,
        )

    for d in range(1, n - 1):
        relay(1, d)
        relay(2, d)

    lane = lax.broadcasted_iota(jnp.int32, (1, wide), 1)
    column = lax.rem(lane, row_width)
    bias = column_of(bias_ref[...])
    for s in range(2):
        relay(1 + s, n - 1)
        pair = gath[1 + s].reshape(channels, packed)
        stack[s, :channels] = pair[:, :wide]
        stack[s, pl.ds(channels, channels)] = second_half(pair, pixels, wide)
        new_ref[s, 0] = stack[s, pl.ds(channels + own, rows), :pixels]
        acc[s] += jnp.dot(
            wcat[:, :, : 2 * channels].reshape(taps, 2 * channels),
            stack[s, : 2 * channels],
            preferred_element_type=jnp.float32,
        )
        total = jnp.zeros((rows, wide), jnp.float32)
        for kx in range(3):
            part = acc[s, pl.ds((3 + kx) * rows, rows)]
            above = pltpu.roll(acc[s, pl.ds(kx * rows, rows)], row_width, axis=1)
            part = part + jnp.where(lane >= row_width, above, 0.0)
            below = pltpu.roll(acc[s, pl.ds((6 + kx) * rows, rows)], wide - row_width, axis=1)
            part = part + jnp.where(lane < pixels - row_width, below, 0.0)
            if kx == 0:
                part = jnp.where(column >= 1, pltpu.roll(part, 1, axis=1), 0.0)
            if kx == 2:
                part = jnp.where(column < row_width - 1, pltpu.roll(part, wide - 1, axis=1), 0.0)
            total = total + part
        result = lat_ref[s, 0].astype(jnp.float32) + (total + bias)[:, :pixels]
        live = jnp.full((rows, pixels), counts_ref[0], jnp.int32) > s
        dec_ref[s, 0] = jnp.where(live, result, 0.0).astype(jnp.bfloat16)

    for copy in moves:
        copy.wait_send()
    for j in range(3):
        for src in range(n):
            @pl.when((me < n - 1) & (src <= me))
            def _():
                up_copy(j, src).wait_send()

            @pl.when((me > 0) & (src >= me))
            def _():
                down_copy(j, src).wait_send()


def shards_kernel(latents, prior_frame_cache, move_to, counts, norm_gain, conv_weight, conv_bias):
    n, ring = lax.axis_size("mp"), lax.axis_size("req")
    rows, pixels = latents.shape[2], latents.shape[3]
    channels = n * rows
    packed, wide = lane_pad(2 * pixels + 1), lane_pad(pixels)
    vmem = pl.BlockSpec(memory_space=pltpu.VMEM)
    smem = pl.BlockSpec(memory_space=pltpu.SMEM)
    return pl.pallas_call(
        functools.partial(block_kernel, n, ring, LATENT_COLUMNS),
        out_shape=(
            jax.ShapeDtypeStruct(latents.shape, jnp.bfloat16),
            jax.ShapeDtypeStruct(prior_frame_cache.shape, jnp.bfloat16),
        ),
        in_specs=[smem, smem, vmem, vmem, vmem, vmem, pl.BlockSpec(memory_space=pl.ANY)],
        out_specs=(vmem, vmem),
        scratch_shapes=[
            pltpu.VMEM((9, rows, 3 * channels), jnp.bfloat16),
            pltpu.VMEM((3, n, rows, packed), jnp.bfloat16),
            pltpu.VMEM((2, rows, packed), jnp.bfloat16),
            pltpu.VMEM((2, rows, packed), jnp.bfloat16),
            pltpu.VMEM((2, 3 * channels, wide), jnp.bfloat16),
            pltpu.VMEM((2, 9 * rows, wide), jnp.float32),
            pltpu.SemaphoreType.DMA((3,)),
            pltpu.SemaphoreType.DMA((2,)),
            pltpu.SemaphoreType.DMA((2,)),
            pltpu.SemaphoreType.DMA((3, n)),
            pltpu.SemaphoreType.DMA((3, n)),
            pltpu.SemaphoreType.DMA((3, n)),
        ],
        compiler_params=pltpu.CompilerParams(
            collective_id=0, has_side_effects=True, vmem_limit_bytes=56 << 20
        ),
    )(
        move_to,
        counts,
        latents,
        prior_frame_cache,
        norm_gain.reshape(1, rows),
        conv_bias.reshape(1, rows),
        conv_weight,
    )


def shards(latents, *rest):
    fits = (
        latents.shape[0] == 2
        and latents.shape[1] == 1
        and latents.shape[2] % 32 == 0
        and lax.axis_size("req") > 2
        and lax.axis_size("mp") > 1
        and lax.axis_size("mp") * latents.shape[2] % 128 == 0
    )
    return (shards_kernel if fits else shards_plain)(latents, *rest)


def solution(mesh):
    in_specs = (
        P("req", None, "mp", None),
        P("req", None, "mp", None),
        P("req"),
        P("req"),
        P("mp"),
        P(None, "mp", None),
        P("mp"),
    )
    out_specs = (P("req", None, "mp", None), P("req", None, "mp", None))
    return jax.shard_map(shards, mesh=mesh, in_specs=in_specs, out_specs=out_specs, check_vma=False)
```

```python
import functools

import jax
import jax.numpy as jnp
from jax import lax
from jax.experimental import pallas as pl
from jax.experimental.pallas import tpu as pltpu
from jax.sharding import PartitionSpec as P

SECTION_CHANNELS = 384
LATENT_COLUMNS = 104


def shifted_2(block, axis, distance):
    devices = range(lax.axis_size(axis))
    route = [((i - distance) % len(devices), i) for i in devices]
    return lax.ppermute(block, axis, route)


def apply_taps(running, shard_in, weights, row_width):
    frames = shard_in.shape[1] - 2
    pixels = shard_in.shape[3]
    padded = jnp.pad(shard_in, ((0, 0), (0, 0), (0, 0), (row_width + 1, row_width + 1)))
    column = jnp.arange(pixels + 2 * row_width) % row_width
    for step_x in range(3):
        inside = ((column + step_x - 1 >= 0) & (column + step_x - 1 < row_width)).astype(
            shard_in.dtype
        )
        shifted = padded[:, :, :, step_x : step_x + pixels + 2 * row_width] * inside
        for step_y in range(3):
            window = shifted[:, :, :, step_y * row_width : step_y * row_width + pixels]
            for step_t in range(3):
                running = running + jnp.einsum(
                    "oc,stcp->stop",
                    weights[step_t * 9 + step_y * 3 + step_x],
                    window[:, step_t : step_t + frames],
                    preferred_element_type=jnp.float32,
                )
    return running


def pack_slots(prior_frame_cache, chosen, target, capacity):
    ranking = jnp.cumsum(chosen.astype(jnp.int32)) - 1
    picker = (chosen[None, :] & (ranking[None, :] == jnp.arange(capacity)[:, None])).astype(
        jnp.bfloat16
    )
    blocks = jnp.einsum(
        "cs,sfkp->cfkp", picker, prior_frame_cache, preferred_element_type=jnp.float32
    ).astype(jnp.bfloat16)
    labels = (jnp.dot(picker.astype(jnp.float32), (target + 1).astype(jnp.float32)) - 1.0).astype(
        jnp.bfloat16
    )
    return (blocks, labels)


def migrate(prior_frame_cache, move_to):
    slot_count = prior_frame_cache.shape[0]
    member_slots = lax.axis_size("req")
    position = lax.axis_index("req")
    capacity = slot_count // 2
    device = move_to // slot_count
    target = move_to % slot_count
    offset = (device - position) % member_slots
    goes_right = offset == 1
    goes_left = offset == member_slots - 1
    stays_put = offset == 0
    blocks_right, labels_right = pack_slots(prior_frame_cache, goes_right, target, capacity)
    blocks_left, labels_left = pack_slots(prior_frame_cache, goes_left, target, capacity)
    from_left = shifted_2((blocks_right, labels_right), "req", 1)
    from_right = shifted_2((blocks_left, labels_left), "req", -1)
    sources = jnp.concatenate([prior_frame_cache, from_left[0], from_right[0]], axis=0)
    own_labels = jnp.where(stays_put, target, -1).astype(jnp.float32)
    labels = jnp.concatenate(
        [own_labels, from_left[1].astype(jnp.float32), from_right[1].astype(jnp.float32)]
    )
    placing = (labels[None, :] == jnp.arange(slot_count, dtype=jnp.float32)[:, None]).astype(
        jnp.bfloat16
    )
    return jnp.einsum("ns,sfkp->nfkp", placing, sources, preferred_element_type=jnp.float32).astype(
        jnp.bfloat16
    )


def normalize(values, squares, gains):
    scaled = (
        values.astype(jnp.float32)
        * lax.rsqrt(squares / SECTION_CHANNELS + 1e-06)
        * gains.astype(jnp.float32)[:, None]
    )
    return jax.nn.silu(scaled).astype(jnp.bfloat16)


def shards_plain(latents, prior_frame_cache, move_to, counts, norm_gain, conv_weight, conv_bias):
    moved = migrate(prior_frame_cache, move_to)
    slot_count = latents.shape[0]
    frames = latents.shape[1]
    live = (jnp.arange(slot_count) < counts[0])[:, None, None, None]
    start_zero = jnp.zeros(
        (slot_count, frames, conv_weight.shape[1], latents.shape[3]), jnp.float32
    )
    values = latents.astype(jnp.float32)
    partial_squares = jnp.sum(values * values, axis=2, keepdims=True)
    squares = lax.psum(partial_squares, "mp")
    hidden = normalize(latents, squares, norm_gain)
    extended = jnp.concatenate([moved, hidden], axis=1)
    conv_sum = apply_taps(
        start_zero, lax.all_gather(extended, "mp", axis=2, tiled=True), conv_weight, LATENT_COLUMNS
    )
    total = latents.astype(jnp.float32) + conv_sum + conv_bias[:, None]
    decoded = jnp.where(live, total, jnp.zeros_like(total)).astype(jnp.bfloat16)
    new_cache = extended[:, frames:]
    return (decoded, new_cache)


MESH = pl.DeviceIdType.MESH


def lane_pad(n):
    return (n + 127) // 128 * 128


def column_of(row):
    n = row.shape[1]
    square = lax.broadcasted_iota(jnp.int32, (n, n), 0) == lax.broadcasted_iota(
        jnp.int32, (n, n), 1
    )
    return jnp.sum(jnp.where(square, jnp.broadcast_to(row, (n, n)), 0.0), axis=1, keepdims=True)


def pack_pair(first, second, extra, packed):
    rows, pixels = first.shape
    tail = jnp.broadcast_to(extra, (rows, packed - 2 * pixels))
    return jnp.concatenate([first, second, tail], axis=1)


def second_half(pair, pixels, wide):
    start = pixels // 128 * 128
    part = pair[:, start : start + wide].astype(jnp.float32)
    return pltpu.roll(part, wide - pixels % 128, axis=1).astype(jnp.bfloat16)


def block_kernel(
    n,
    ring,
    row_width,
    move_ref,
    counts_ref,
    lat_ref,
    cache_ref,
    gain_ref,
    bias_ref,
    w_ref,
    dec_ref,
    new_ref,
    wcat,
    gath,
    last,
    mig_out,
    mig_in,
    stack,
    acc,
    w_sem,
    mig_send,
    mig_recv,
    up_send,
    down_send,
    ag_recv,
):
    me = lax.axis_index("mp")
    pos = lax.axis_index("req")
    rows, pixels = lat_ref.shape[2], lat_ref.shape[3]
    packed = gath.shape[3]
    wide = stack.shape[2]
    channels = n * rows
    right, left = lax.rem(pos + 1, ring), lax.rem(pos + ring - 1, ring)

    w_copies = []
    for kt in range(3):
        copy = pltpu.make_async_copy(
            w_ref.at[pl.ds(9 * kt, 9)],
            wcat.at[:, :, pl.ds(channels * kt, channels)],
            w_sem.at[kt],
        )
        copy.start()
        w_copies.append(copy)

    barrier = pltpu.get_barrier_semaphore()
    for neighbour in (right, left):
        pl.semaphore_signal(barrier, inc=1, device_id={"req": neighbour}, device_id_type=MESH)

    @pl.when(me < n - 1)
    def _():
        pl.semaphore_signal(barrier, inc=1, device_id={"mp": me + 1}, device_id_type=MESH)

    @pl.when(me > 0)
    def _():
        pl.semaphore_signal(barrier, inc=1, device_id={"mp": me - 1}, device_id_type=MESH)

    gain = column_of(gain_ref[...].astype(jnp.float32))
    gath[0, me] = pack_pair(
        lat_ref[0, 0].astype(jnp.float32), lat_ref[1, 0].astype(jnp.float32), gain, packed
    ).astype(jnp.bfloat16)

    inner = (me > 0) & (me < n - 1)

    @pl.when(inner)
    def _():
        pl.semaphore_wait(barrier, 4)

    @pl.when(jnp.logical_not(inner))
    def _():
        pl.semaphore_wait(barrier, 3)

    half = rows // 2

    def piece(j, src):
        if j < 2:
            return gath.at[0, src, pl.ds(half * j, half)]
        return gath.at[1, src] if j == 2 else last.at[src]

    def up_copy(j, src):
        return pltpu.make_async_remote_copy(
            src_ref=piece(j, src),
            dst_ref=piece(j, src),
            send_sem=up_send.at[j, src],
            recv_sem=ag_recv.at[j, src],
            device_id={"mp": me + 1},
            device_id_type=MESH,
        )

    def down_copy(j, src):
        return pltpu.make_async_remote_copy(
            src_ref=piece(j, src),
            dst_ref=piece(j, src),
            send_sem=down_send.at[j, src],
            recv_sem=ag_recv.at[j, src],
            device_id={"mp": me - 1},
            device_id_type=MESH,
        )

    def send_own(j):
        @pl.when(me < n - 1)
        def _():
            up_copy(j, me).start()

        @pl.when(me > 0)
        def _():
            down_copy(j, me).start()

    def relay(j, d):
        @pl.when(me - d >= 0)
        def _():
            down_copy(j, me - d).wait_recv()

            @pl.when(me < n - 1)
            def _():
                up_copy(j, me - d).start()

        @pl.when(me + d <= n - 1)
        def _():
            up_copy(j, me + d).wait_recv()

            @pl.when(me > 0)
            def _():
                down_copy(j, me + d).start()

    send_own(0)
    send_own(1)

    slots = lat_ref.shape[0]
    offset = lax.rem(lax.div(move_ref[0], slots) - pos + ring, ring)
    first_right = jnp.where(offset == 1, 1.0, 0.0).astype(jnp.float32)
    pairs = []
    for s in range(2):
        label = jnp.full((rows, 1), lax.rem(move_ref[s], slots), jnp.int32).astype(jnp.float32)
        pairs.append(
            pack_pair(
                cache_ref[s, 0].astype(jnp.float32),
                cache_ref[s, 1].astype(jnp.float32),
                label,
                packed,
            )
        )
    pick = jnp.full((rows, packed), first_right, jnp.float32) > 0.5
    mig_out[0] = jnp.where(pick, pairs[0], pairs[1]).astype(jnp.bfloat16)
    mig_out[1] = jnp.where(pick, pairs[1], pairs[0]).astype(jnp.bfloat16)
    moves = []
    for k, neighbour in enumerate((right, left)):
        copy = pltpu.make_async_remote_copy(
            src_ref=mig_out.at[k],
            dst_ref=mig_in.at[k],
            send_sem=mig_send.at[k],
            recv_sem=mig_recv.at[k],
            device_id={"req": neighbour},
            device_id_type=MESH,
        )
        copy.start()
        moves.append(copy)

    relay(0, 1)
    relay(1, 1)
    for copy in moves:
        copy.wait_recv()
    from_left = mig_in[0].astype(jnp.float32)
    from_right = mig_in[1].astype(jnp.float32)
    to_second = jnp.broadcast_to(from_left[:, 2 * pixels : 2 * pixels + 1], (rows, packed)) > 0.5
    slot_0 = jnp.where(to_second, from_right, from_left)
    slot_1 = jnp.where(to_second, from_left, from_right)
    spill = packed - 2 * pixels
    turned = pltpu.roll(slot_1, packed - spill, axis=1)
    spare = lax.broadcasted_iota(jnp.int32, (rows, packed), 1) >= 2 * pixels
    gath[1, me] = jnp.where(spare, turned, slot_0).astype(jnp.bfloat16)
    last[me] = turned[:, : packed - 128].astype(jnp.bfloat16)
    send_own(2)
    send_own(3)
    for d in range(2, n):
        relay(0, d)
        relay(1, d)

    own = pl.multiple_of(me * rows, rows)
    values = gath[0].reshape(channels, packed).astype(jnp.float32)
    gains = values[:, 2 * pixels : 2 * pixels + 1]
    squares = jnp.sum(values * values, axis=0, keepdims=True)
    scaled = values * lax.rsqrt(squares / channels + 1e-06) * gains
    hidden = (scaled / (1.0 + jnp.exp(-scaled))).astype(jnp.bfloat16)
    stack[0, pl.ds(2 * channels, channels)] = hidden[:, :wide]
    stack[1, pl.ds(2 * channels, channels)] = second_half(hidden, pixels, wide)
    for copy in w_copies:
        copy.wait()
    taps = 9 * rows
    for s in range(2):
        new_ref[s, 1] = stack[s, pl.ds(2 * channels + own, rows), :pixels]
        acc[s] = jnp.dot(
            wcat[:, :, 2 * channels :].reshape(taps, channels),
            stack[s, pl.ds(2 * channels, channels)],
            preferred_element_type=jnp.float32,
        )

    for d in range(1, n - 1):
        relay(2, d)
        relay(3, d)

    lane = lax.broadcasted_iota(jnp.int32, (1, wide), 1)
    column = lax.rem(lane, row_width)
    bias = column_of(bias_ref[...])
    for s in range(2):
        relay(2 + s, n - 1)
        pair = gath[1].reshape(channels, packed)
        if s == 1:
            rest = last[...].reshape(channels, packed - 128).astype(jnp.float32)
            head = pair[:, packed - 128 :].astype(jnp.float32)
            pair = jnp.concatenate([rest, head], axis=1)
            pair = pltpu.roll(pair, spill, axis=1).astype(jnp.bfloat16)
        stack[s, :channels] = pair[:, :wide]
        stack[s, pl.ds(channels, channels)] = second_half(pair, pixels, wide)
        new_ref[s, 0] = stack[s, pl.ds(channels + own, rows), :pixels]
        acc[s] += jnp.dot(
            wcat[:, :, : 2 * channels].reshape(taps, 2 * channels),
            stack[s, : 2 * channels],
            preferred_element_type=jnp.float32,
        )
        total = jnp.zeros((rows, wide), jnp.float32)
        for kx in range(3):
            part = acc[s, pl.ds((3 + kx) * rows, rows)]
            above = pltpu.roll(acc[s, pl.ds(kx * rows, rows)], row_width, axis=1)
            part = part + jnp.where(lane >= row_width, above, 0.0)
            below = pltpu.roll(acc[s, pl.ds((6 + kx) * rows, rows)], wide - row_width, axis=1)
            part = part + jnp.where(lane < pixels - row_width, below, 0.0)
            if kx == 0:
                part = jnp.where(column >= 1, pltpu.roll(part, 1, axis=1), 0.0)
            if kx == 2:
                part = jnp.where(column < row_width - 1, pltpu.roll(part, wide - 1, axis=1), 0.0)
            total = total + part
        result = lat_ref[s, 0].astype(jnp.float32) + (total + bias)[:, :pixels]
        live = jnp.full((rows, pixels), counts_ref[0], jnp.int32) > s
        dec_ref[s, 0] = jnp.where(live, result, 0.0).astype(jnp.bfloat16)

    for copy in moves:
        copy.wait_send()
    for j in range(4):
        for src in range(n):
            @pl.when((me < n - 1) & (src <= me))
            def _():
                up_copy(j, src).wait_send()

            @pl.when((me > 0) & (src >= me))
            def _():
                down_copy(j, src).wait_send()


def place_kernel(dec_ref, new_ref, dec_out, new_out):
    dec_out[...] = dec_ref[...]
    new_out[...] = new_ref[...]


def shards_kernel(latents, prior_frame_cache, move_to, counts, norm_gain, conv_weight, conv_bias):
    n, ring = lax.axis_size("mp"), lax.axis_size("req")
    rows, pixels = latents.shape[2], latents.shape[3]
    channels = n * rows
    packed, wide = lane_pad(2 * pixels + 1), lane_pad(pixels)
    vmem = pl.BlockSpec(memory_space=pltpu.VMEM)
    smem = pl.BlockSpec(memory_space=pltpu.SMEM)
    results = pl.pallas_call(
        functools.partial(block_kernel, n, ring, LATENT_COLUMNS),
        out_shape=(
            jax.ShapeDtypeStruct(latents.shape, jnp.bfloat16),
            jax.ShapeDtypeStruct(prior_frame_cache.shape, jnp.bfloat16),
        ),
        in_specs=[smem, smem, vmem, vmem, vmem, vmem, pl.BlockSpec(memory_space=pltpu.HBM)],
        out_specs=(vmem, vmem),
        scratch_shapes=[
            pltpu.VMEM((9, rows, 3 * channels), jnp.bfloat16),
            pltpu.VMEM((2, n, rows, packed), jnp.bfloat16),
            pltpu.VMEM((n, rows, packed - 128), jnp.bfloat16),
            pltpu.VMEM((2, rows, packed), jnp.bfloat16),
            pltpu.VMEM((2, rows, packed), jnp.bfloat16),
            pltpu.VMEM((2, 3 * channels, wide), jnp.bfloat16),
            pltpu.VMEM((2, 9 * rows, wide), jnp.float32),
            pltpu.SemaphoreType.DMA((3,)),
            pltpu.SemaphoreType.DMA((2,)),
            pltpu.SemaphoreType.DMA((2,)),
            pltpu.SemaphoreType.DMA((4, n)),
            pltpu.SemaphoreType.DMA((4, n)),
            pltpu.SemaphoreType.DMA((4, n)),
        ],
        compiler_params=pltpu.CompilerParams(
            collective_id=0, has_side_effects=True, vmem_limit_bytes=40 << 20
        ),
    )(
        move_to,
        counts,
        latents,
        prior_frame_cache,
        norm_gain.reshape(1, rows),
        conv_bias.reshape(1, rows),
        conv_weight,
    )
    return pl.pallas_call(
        place_kernel,
        out_shape=tuple(jax.ShapeDtypeStruct(r.shape, r.dtype) for r in results),
        in_specs=[vmem, vmem],
        out_specs=(vmem, vmem),
        compiler_params=pltpu.CompilerParams(vmem_limit_bytes=8 << 20),
    )(*results)


def shards(latents, *rest):
    fits = (
        latents.shape[0] == 2
        and latents.shape[1] == 1
        and latents.shape[2] % 32 == 0
        and latents.shape[3] % 128 == 32
        and lax.axis_size("req") > 2
        and lax.axis_size("mp") > 1
        and lax.axis_size("mp") * latents.shape[2] % 128 == 0
    )
    return (shards_kernel if fits else shards_plain)(latents, *rest)


def solution(mesh):
    in_specs = (
        P("req", None, "mp", None),
        P("req", None, "mp", None),
        P("req"),
        P("req"),
        P("mp"),
        P(None, "mp", None),
        P("mp"),
    )
    out_specs = (P("req", None, "mp", None), P("req", None, "mp", None))
    return jax.shard_map(shards, mesh=mesh, in_specs=in_specs, out_specs=out_specs, check_vma=False)
```

```python
import functools

import jax
import jax.numpy as jnp
from jax import lax
from jax.experimental import pallas as pl
from jax.experimental.pallas import tpu as pltpu
from jax.sharding import PartitionSpec as P

SECTION_CHANNELS = 384
LATENT_COLUMNS = 104


def shifted_2(block, axis, distance):
    devices = range(lax.axis_size(axis))
    route = [((i - distance) % len(devices), i) for i in devices]
    return lax.ppermute(block, axis, route)


def apply_taps(running, shard_in, weights, row_width):
    frames = shard_in.shape[1] - 2
    pixels = shard_in.shape[3]
    padded = jnp.pad(shard_in, ((0, 0), (0, 0), (0, 0), (row_width + 1, row_width + 1)))
    column = jnp.arange(pixels + 2 * row_width) % row_width
    for step_x in range(3):
        inside = ((column + step_x - 1 >= 0) & (column + step_x - 1 < row_width)).astype(
            shard_in.dtype
        )
        shifted = padded[:, :, :, step_x : step_x + pixels + 2 * row_width] * inside
        for step_y in range(3):
            window = shifted[:, :, :, step_y * row_width : step_y * row_width + pixels]
            for step_t in range(3):
                running = running + jnp.einsum(
                    "oc,stcp->stop",
                    weights[step_t * 9 + step_y * 3 + step_x],
                    window[:, step_t : step_t + frames],
                    preferred_element_type=jnp.float32,
                )
    return running


def pack_slots(prior_frame_cache, chosen, target, capacity):
    ranking = jnp.cumsum(chosen.astype(jnp.int32)) - 1
    picker = (chosen[None, :] & (ranking[None, :] == jnp.arange(capacity)[:, None])).astype(
        jnp.bfloat16
    )
    blocks = jnp.einsum(
        "cs,sfkp->cfkp", picker, prior_frame_cache, preferred_element_type=jnp.float32
    ).astype(jnp.bfloat16)
    labels = (jnp.dot(picker.astype(jnp.float32), (target + 1).astype(jnp.float32)) - 1.0).astype(
        jnp.bfloat16
    )
    return (blocks, labels)


def migrate(prior_frame_cache, move_to):
    slot_count = prior_frame_cache.shape[0]
    member_slots = lax.axis_size("req")
    position = lax.axis_index("req")
    capacity = slot_count // 2
    device = move_to // slot_count
    target = move_to % slot_count
    offset = (device - position) % member_slots
    goes_right = offset == 1
    goes_left = offset == member_slots - 1
    stays_put = offset == 0
    blocks_right, labels_right = pack_slots(prior_frame_cache, goes_right, target, capacity)
    blocks_left, labels_left = pack_slots(prior_frame_cache, goes_left, target, capacity)
    from_left = shifted_2((blocks_right, labels_right), "req", 1)
    from_right = shifted_2((blocks_left, labels_left), "req", -1)
    sources = jnp.concatenate([prior_frame_cache, from_left[0], from_right[0]], axis=0)
    own_labels = jnp.where(stays_put, target, -1).astype(jnp.float32)
    labels = jnp.concatenate(
        [own_labels, from_left[1].astype(jnp.float32), from_right[1].astype(jnp.float32)]
    )
    placing = (labels[None, :] == jnp.arange(slot_count, dtype=jnp.float32)[:, None]).astype(
        jnp.bfloat16
    )
    return jnp.einsum("ns,sfkp->nfkp", placing, sources, preferred_element_type=jnp.float32).astype(
        jnp.bfloat16
    )


def normalize(values, squares, gains):
    scaled = (
        values.astype(jnp.float32)
        * lax.rsqrt(squares / SECTION_CHANNELS + 1e-06)
        * gains.astype(jnp.float32)[:, None]
    )
    return jax.nn.silu(scaled).astype(jnp.bfloat16)


def shards_plain(latents, prior_frame_cache, move_to, counts, norm_gain, conv_weight, conv_bias):
    moved = migrate(prior_frame_cache, move_to)
    slot_count = latents.shape[0]
    frames = latents.shape[1]
    live = (jnp.arange(slot_count) < counts[0])[:, None, None, None]
    start_zero = jnp.zeros(
        (slot_count, frames, conv_weight.shape[1], latents.shape[3]), jnp.float32
    )
    values = latents.astype(jnp.float32)
    partial_squares = jnp.sum(values * values, axis=2, keepdims=True)
    squares = lax.psum(partial_squares, "mp")
    hidden = normalize(latents, squares, norm_gain)
    extended = jnp.concatenate([moved, hidden], axis=1)
    conv_sum = apply_taps(
        start_zero, lax.all_gather(extended, "mp", axis=2, tiled=True), conv_weight, LATENT_COLUMNS
    )
    total = latents.astype(jnp.float32) + conv_sum + conv_bias[:, None]
    decoded = jnp.where(live, total, jnp.zeros_like(total)).astype(jnp.bfloat16)
    new_cache = extended[:, frames:]
    return (decoded, new_cache)


MESH = pl.DeviceIdType.MESH


def lane_pad(n):
    return (n + 127) // 128 * 128


def column_of(row):
    n = row.shape[1]
    square = lax.broadcasted_iota(jnp.int32, (n, n), 0) == lax.broadcasted_iota(
        jnp.int32, (n, n), 1
    )
    return jnp.sum(jnp.where(square, jnp.broadcast_to(row, (n, n)), 0.0), axis=1, keepdims=True)


def pack_pair(first, second, extra, packed):
    rows, pixels = first.shape
    tail = jnp.broadcast_to(extra, (rows, packed - 2 * pixels))
    return jnp.concatenate([first, second, tail], axis=1)


def second_half(pair, pixels, wide):
    start = pixels // 128 * 128
    part = pair[:, start : start + wide].astype(jnp.float32)
    return pltpu.roll(part, wide - pixels % 128, axis=1).astype(jnp.bfloat16)


def block_kernel(
    n,
    ring,
    row_width,
    move_ref,
    counts_ref,
    lat_ref,
    cache_ref,
    gain_ref,
    bias_ref,
    w_ref,
    dec_ref,
    new_ref,
    wcat,
    gath,
    last,
    mig_out,
    mig_in,
    stack,
    acc,
    w_sem,
    mig_send,
    mig_recv,
    up_send,
    down_send,
    ag_recv,
):
    me = lax.axis_index("mp")
    pos = lax.axis_index("req")
    rows, pixels = lat_ref.shape[2], lat_ref.shape[3]
    packed = gath.shape[3]
    wide = stack.shape[2]
    channels = n * rows
    right, left = lax.rem(pos + 1, ring), lax.rem(pos + ring - 1, ring)

    w_copies = []
    for kt in range(3):
        copy = pltpu.make_async_copy(
            w_ref.at[pl.ds(9 * kt, 9)],
            wcat.at[:, :, pl.ds(channels * kt, channels)],
            w_sem.at[kt],
        )
        copy.start()
        w_copies.append(copy)

    barrier = pltpu.get_barrier_semaphore()
    for neighbour in (right, left):
        pl.semaphore_signal(barrier, inc=1, device_id={"req": neighbour}, device_id_type=MESH)

    @pl.when(me < n - 1)
    def _():
        pl.semaphore_signal(barrier, inc=1, device_id={"mp": me + 1}, device_id_type=MESH)

    @pl.when(me > 0)
    def _():
        pl.semaphore_signal(barrier, inc=1, device_id={"mp": me - 1}, device_id_type=MESH)

    gain = column_of(gain_ref[...].astype(jnp.float32))
    gath[0, me] = pack_pair(
        lat_ref[0, 0].astype(jnp.float32), lat_ref[1, 0].astype(jnp.float32), gain, packed
    ).astype(jnp.bfloat16)

    inner = (me > 0) & (me < n - 1)

    @pl.when(inner)
    def _():
        pl.semaphore_wait(barrier, 4)

    @pl.when(jnp.logical_not(inner))
    def _():
        pl.semaphore_wait(barrier, 3)

    half = rows // 2

    def piece(j, src):
        if j < 2:
            return gath.at[0, src, pl.ds(half * j, half)]
        return gath.at[1, src] if j == 2 else last.at[src]

    def up_copy(j, src):
        return pltpu.make_async_remote_copy(
            src_ref=piece(j, src),
            dst_ref=piece(j, src),
            send_sem=up_send.at[j, src],
            recv_sem=ag_recv.at[j, src],
            device_id={"mp": me + 1},
            device_id_type=MESH,
        )

    def down_copy(j, src):
        return pltpu.make_async_remote_copy(
            src_ref=piece(j, src),
            dst_ref=piece(j, src),
            send_sem=down_send.at[j, src],
            recv_sem=ag_recv.at[j, src],
            device_id={"mp": me - 1},
            device_id_type=MESH,
        )

    def send_own(j):
        @pl.when(me < n - 1)
        def _():
            up_copy(j, me).start()

        @pl.when(me > 0)
        def _():
            down_copy(j, me).start()

    def relay(j, d):
        @pl.when(me - d >= 0)
        def _():
            down_copy(j, me - d).wait_recv()

            @pl.when(me < n - 1)
            def _():
                up_copy(j, me - d).start()

        @pl.when(me + d <= n - 1)
        def _():
            up_copy(j, me + d).wait_recv()

            @pl.when(me > 0)
            def _():
                down_copy(j, me + d).start()

    send_own(0)
    send_own(1)

    slots = lat_ref.shape[0]
    offset = lax.rem(lax.div(move_ref[0], slots) - pos + ring, ring)
    first_right = jnp.where(offset == 1, 1.0, 0.0).astype(jnp.float32)
    pairs = []
    for s in range(2):
        label = jnp.full((rows, 1), lax.rem(move_ref[s], slots), jnp.int32).astype(jnp.float32)
        pairs.append(
            pack_pair(
                cache_ref[s, 0].astype(jnp.float32),
                cache_ref[s, 1].astype(jnp.float32),
                label,
                packed,
            )
        )
    pick = jnp.full((rows, packed), first_right, jnp.float32) > 0.5
    mig_out[0] = jnp.where(pick, pairs[0], pairs[1]).astype(jnp.bfloat16)
    mig_out[1] = jnp.where(pick, pairs[1], pairs[0]).astype(jnp.bfloat16)
    moves = []
    for k, neighbour in enumerate((right, left)):
        copy = pltpu.make_async_remote_copy(
            src_ref=mig_out.at[k],
            dst_ref=mig_in.at[k],
            send_sem=mig_send.at[k],
            recv_sem=mig_recv.at[k],
            device_id={"req": neighbour},
            device_id_type=MESH,
        )
        copy.start()
        moves.append(copy)

    relay(0, 1)
    relay(1, 1)
    for copy in moves:
        copy.wait_recv()
    from_left = mig_in[0].astype(jnp.float32)
    from_right = mig_in[1].astype(jnp.float32)
    to_second = jnp.broadcast_to(from_left[:, 2 * pixels : 2 * pixels + 1], (rows, packed)) > 0.5
    slot_0 = jnp.where(to_second, from_right, from_left)
    slot_1 = jnp.where(to_second, from_left, from_right)
    spill = packed - 2 * pixels
    turned = pltpu.roll(slot_1, packed - spill, axis=1)
    spare = lax.broadcasted_iota(jnp.int32, (rows, packed), 1) >= 2 * pixels
    gath[1, me] = jnp.where(spare, turned, slot_0).astype(jnp.bfloat16)
    last[me] = turned[:, : packed - 128].astype(jnp.bfloat16)
    send_own(2)
    send_own(3)
    for d in range(2, n):
        relay(0, d)
        relay(1, d)

    own = pl.multiple_of(me * rows, rows)
    values = gath[0].reshape(channels, packed).astype(jnp.float32)
    gains = values[:, 2 * pixels : 2 * pixels + 1]
    squares = jnp.sum(values * values, axis=0, keepdims=True)
    scaled = values * lax.rsqrt(squares / channels + 1e-06) * gains
    hidden = (scaled / (1.0 + jnp.exp(-scaled))).astype(jnp.bfloat16)
    stack[0, pl.ds(2 * channels, channels)] = hidden[:, :wide]
    stack[1, pl.ds(2 * channels, channels)] = second_half(hidden, pixels, wide)
    for copy in w_copies:
        copy.wait()
    taps = 9 * rows
    for s in range(2):
        new_ref[s, 1] = stack[s, pl.ds(2 * channels + own, rows), :pixels]
        acc[s] = jnp.dot(
            wcat[:, :, 2 * channels :].reshape(taps, channels),
            stack[s, pl.ds(2 * channels, channels)],
            preferred_element_type=jnp.float32,
        )

    for d in range(1, n - 1):
        relay(2, d)
        relay(3, d)

    lane = lax.broadcasted_iota(jnp.int32, (1, wide), 1)
    column = lax.rem(lane, row_width)
    bias = column_of(bias_ref[...])
    for s in range(2):
        relay(2 + s, n - 1)
        pair = gath[1].reshape(channels, packed)
        if s == 1:
            rest = last[...].reshape(channels, packed - 128).astype(jnp.float32)
            head = pair[:, packed - 128 :].astype(jnp.float32)
            pair = jnp.concatenate([rest, head], axis=1)
            pair = pltpu.roll(pair, spill, axis=1).astype(jnp.bfloat16)
        stack[s, :channels] = pair[:, :wide]
        stack[s, pl.ds(channels, channels)] = second_half(pair, pixels, wide)
        new_ref[s, 0] = stack[s, pl.ds(channels + own, rows), :pixels]
        acc[s] += jnp.dot(
            wcat[:, :, : 2 * channels].reshape(taps, 2 * channels),
            stack[s, : 2 * channels],
            preferred_element_type=jnp.float32,
        )
        total = jnp.zeros((rows, wide), jnp.float32)
        for kx in range(3):
            part = acc[s, pl.ds((3 + kx) * rows, rows)]
            above = pltpu.roll(acc[s, pl.ds(kx * rows, rows)], row_width, axis=1)
            part = part + jnp.where(lane >= row_width, above, 0.0)
            below = pltpu.roll(acc[s, pl.ds((6 + kx) * rows, rows)], wide - row_width, axis=1)
            part = part + jnp.where(lane < pixels - row_width, below, 0.0)
            if kx == 0:
                part = jnp.where(column >= 1, pltpu.roll(part, 1, axis=1), 0.0)
            if kx == 2:
                part = jnp.where(column < row_width - 1, pltpu.roll(part, wide - 1, axis=1), 0.0)
            total = total + part
        result = lat_ref[s, 0].astype(jnp.float32) + (total + bias)[:, :pixels]
        live = jnp.full((rows, pixels), counts_ref[0], jnp.int32) > s
        dec_ref[s, 0] = jnp.where(live, result, 0.0).astype(jnp.bfloat16)

    for copy in moves:
        copy.wait_send()
    for j in range(4):
        for src in range(n):
            @pl.when((me < n - 1) & (src <= me))
            def _():
                up_copy(j, src).wait_send()

            @pl.when((me > 0) & (src >= me))
            def _():
                down_copy(j, src).wait_send()


def place_kernel(dec_ref, new_ref, dec_out, new_out):
    dec_out[...] = dec_ref[...]
    new_out[...] = new_ref[...]


def shards_kernel(latents, prior_frame_cache, move_to, counts, norm_gain, conv_weight, conv_bias):
    n, ring = lax.axis_size("mp"), lax.axis_size("req")
    rows, pixels = latents.shape[2], latents.shape[3]
    channels = n * rows
    packed, wide = lane_pad(2 * pixels + 1), lane_pad(pixels)
    vmem = pl.BlockSpec(memory_space=pltpu.VMEM)
    smem = pl.BlockSpec(memory_space=pltpu.SMEM)
    results = pl.pallas_call(
        functools.partial(block_kernel, n, ring, LATENT_COLUMNS),
        out_shape=(
            pltpu.VMEM(latents.shape, jnp.bfloat16),
            pltpu.VMEM(prior_frame_cache.shape, jnp.bfloat16),
        ),
        in_specs=[smem, smem, vmem, vmem, vmem, vmem, pl.BlockSpec(memory_space=pltpu.HBM)],
        out_specs=(vmem, vmem),
        scratch_shapes=[
            pltpu.VMEM((9, rows, 3 * channels), jnp.bfloat16),
            pltpu.VMEM((2, n, rows, packed), jnp.bfloat16),
            pltpu.VMEM((n, rows, packed - 128), jnp.bfloat16),
            pltpu.VMEM((2, rows, packed), jnp.bfloat16),
            pltpu.VMEM((2, rows, packed), jnp.bfloat16),
            pltpu.VMEM((2, 3 * channels, wide), jnp.bfloat16),
            pltpu.VMEM((2, 9 * rows, wide), jnp.float32),
            pltpu.SemaphoreType.DMA((3,)),
            pltpu.SemaphoreType.DMA((2,)),
            pltpu.SemaphoreType.DMA((2,)),
            pltpu.SemaphoreType.DMA((4, n)),
            pltpu.SemaphoreType.DMA((4, n)),
            pltpu.SemaphoreType.DMA((4, n)),
        ],
        compiler_params=pltpu.CompilerParams(
            collective_id=0, has_side_effects=True, vmem_limit_bytes=63 << 20
        ),
    )(
        move_to,
        counts,
        latents,
        prior_frame_cache,
        norm_gain.reshape(1, rows),
        conv_bias.reshape(1, rows),
        conv_weight,
    )
    return pl.pallas_call(
        place_kernel,
        out_shape=tuple(jax.ShapeDtypeStruct(r.shape, r.dtype) for r in results),
        in_specs=[vmem, vmem],
        out_specs=(vmem, vmem),
        compiler_params=pltpu.CompilerParams(vmem_limit_bytes=8 << 20),
    )(*results)


def shards(latents, *rest):
    fits = (
        latents.shape[0] == 2
        and latents.shape[1] == 1
        and latents.shape[2] % 32 == 0
        and latents.shape[3] % 128 == 32
        and lax.axis_size("req") > 2
        and lax.axis_size("mp") > 1
        and lax.axis_size("mp") * latents.shape[2] % 128 == 0
    )
    return (shards_kernel if fits else shards_plain)(latents, *rest)


def solution(mesh):
    in_specs = (
        P("req", None, "mp", None),
        P("req", None, "mp", None),
        P("req"),
        P("req"),
        P("mp"),
        P(None, "mp", None),
        P("mp"),
    )
    out_specs = (P("req", None, "mp", None), P("req", None, "mp", None))
    return jax.shard_map(shards, mesh=mesh, in_specs=in_specs, out_specs=out_specs, check_vma=False)
```

```python
import functools

import jax
import jax.numpy as jnp
from jax import lax
from jax.experimental import pallas as pl
from jax.experimental.pallas import tpu as pltpu
from jax.sharding import PartitionSpec as P

SECTION_CHANNELS = 384
LATENT_COLUMNS = 104


def shifted_2(block, axis, distance):
    devices = range(lax.axis_size(axis))
    route = [((i - distance) % len(devices), i) for i in devices]
    return lax.ppermute(block, axis, route)


def apply_taps(running, shard_in, weights, row_width):
    frames = shard_in.shape[1] - 2
    pixels = shard_in.shape[3]
    padded = jnp.pad(shard_in, ((0, 0), (0, 0), (0, 0), (row_width + 1, row_width + 1)))
    column = jnp.arange(pixels + 2 * row_width) % row_width
    for step_x in range(3):
        inside = ((column + step_x - 1 >= 0) & (column + step_x - 1 < row_width)).astype(
            shard_in.dtype
        )
        shifted = padded[:, :, :, step_x : step_x + pixels + 2 * row_width] * inside
        for step_y in range(3):
            window = shifted[:, :, :, step_y * row_width : step_y * row_width + pixels]
            for step_t in range(3):
                running = running + jnp.einsum(
                    "oc,stcp->stop",
                    weights[step_t * 9 + step_y * 3 + step_x],
                    window[:, step_t : step_t + frames],
                    preferred_element_type=jnp.float32,
                )
    return running


def pack_slots(prior_frame_cache, chosen, target, capacity):
    ranking = jnp.cumsum(chosen.astype(jnp.int32)) - 1
    picker = (chosen[None, :] & (ranking[None, :] == jnp.arange(capacity)[:, None])).astype(
        jnp.bfloat16
    )
    blocks = jnp.einsum(
        "cs,sfkp->cfkp", picker, prior_frame_cache, preferred_element_type=jnp.float32
    ).astype(jnp.bfloat16)
    labels = (jnp.dot(picker.astype(jnp.float32), (target + 1).astype(jnp.float32)) - 1.0).astype(
        jnp.bfloat16
    )
    return (blocks, labels)


def migrate(prior_frame_cache, move_to):
    slot_count = prior_frame_cache.shape[0]
    member_slots = lax.axis_size("req")
    position = lax.axis_index("req")
    capacity = slot_count // 2
    device = move_to // slot_count
    target = move_to % slot_count
    offset = (device - position) % member_slots
    goes_right = offset == 1
    goes_left = offset == member_slots - 1
    stays_put = offset == 0
    blocks_right, labels_right = pack_slots(prior_frame_cache, goes_right, target, capacity)
    blocks_left, labels_left = pack_slots(prior_frame_cache, goes_left, target, capacity)
    from_left = shifted_2((blocks_right, labels_right), "req", 1)
    from_right = shifted_2((blocks_left, labels_left), "req", -1)
    sources = jnp.concatenate([prior_frame_cache, from_left[0], from_right[0]], axis=0)
    own_labels = jnp.where(stays_put, target, -1).astype(jnp.float32)
    labels = jnp.concatenate(
        [own_labels, from_left[1].astype(jnp.float32), from_right[1].astype(jnp.float32)]
    )
    placing = (labels[None, :] == jnp.arange(slot_count, dtype=jnp.float32)[:, None]).astype(
        jnp.bfloat16
    )
    return jnp.einsum("ns,sfkp->nfkp", placing, sources, preferred_element_type=jnp.float32).astype(
        jnp.bfloat16
    )


def normalize(values, squares, gains):
    scaled = (
        values.astype(jnp.float32)
        * lax.rsqrt(squares / SECTION_CHANNELS + 1e-06)
        * gains.astype(jnp.float32)[:, None]
    )
    return jax.nn.silu(scaled).astype(jnp.bfloat16)


def shards_plain(latents, prior_frame_cache, move_to, counts, norm_gain, conv_weight, conv_bias):
    moved = migrate(prior_frame_cache, move_to)
    slot_count = latents.shape[0]
    frames = latents.shape[1]
    live = (jnp.arange(slot_count) < counts[0])[:, None, None, None]
    start_zero = jnp.zeros(
        (slot_count, frames, conv_weight.shape[1], latents.shape[3]), jnp.float32
    )
    values = latents.astype(jnp.float32)
    partial_squares = jnp.sum(values * values, axis=2, keepdims=True)
    squares = lax.psum(partial_squares, "mp")
    hidden = normalize(latents, squares, norm_gain)
    extended = jnp.concatenate([moved, hidden], axis=1)
    conv_sum = apply_taps(
        start_zero, lax.all_gather(extended, "mp", axis=2, tiled=True), conv_weight, LATENT_COLUMNS
    )
    total = latents.astype(jnp.float32) + conv_sum + conv_bias[:, None]
    decoded = jnp.where(live, total, jnp.zeros_like(total)).astype(jnp.bfloat16)
    new_cache = extended[:, frames:]
    return (decoded, new_cache)


MESH = pl.DeviceIdType.MESH


def lane_pad(n):
    return (n + 127) // 128 * 128


def column_of(row):
    n = row.shape[1]
    square = lax.broadcasted_iota(jnp.int32, (n, n), 0) == lax.broadcasted_iota(
        jnp.int32, (n, n), 1
    )
    return jnp.sum(jnp.where(square, jnp.broadcast_to(row, (n, n)), 0.0), axis=1, keepdims=True)


def pack_pair(first, second, extra, packed):
    rows, pixels = first.shape
    tail = jnp.broadcast_to(extra, (rows, packed - 2 * pixels))
    return jnp.concatenate([first, second, tail], axis=1)


def second_half(pair, pixels, wide):
    start = pixels // 128 * 128
    part = pair[:, start : start + wide].astype(jnp.float32)
    return pltpu.roll(part, wide - pixels % 128, axis=1).astype(jnp.bfloat16)


def block_kernel(
    n,
    ring,
    row_width,
    move_ref,
    counts_ref,
    lat_ref,
    cache_ref,
    gain_ref,
    bias_ref,
    w_ref,
    dec_ref,
    new_ref,
    wcat,
    gath,
    last,
    mig_out,
    mig_in,
    stack,
    acc,
    w_sem,
    mig_send,
    mig_recv,
    up_send,
    down_send,
    ag_recv,
):
    me = lax.axis_index("mp")
    pos = lax.axis_index("req")
    rows, pixels = lat_ref.shape[2], lat_ref.shape[3]
    packed = gath.shape[3]
    wide = stack.shape[2]
    channels = n * rows
    right, left = lax.rem(pos + 1, ring), lax.rem(pos + ring - 1, ring)

    w_copies = []
    for kt in range(3):
        copy = pltpu.make_async_copy(
            w_ref.at[pl.ds(9 * kt, 9)],
            wcat.at[:, :, pl.ds(channels * kt, channels)],
            w_sem.at[kt],
        )
        copy.start()
        w_copies.append(copy)

    barrier = pltpu.get_barrier_semaphore()
    for neighbour in (right, left):
        pl.semaphore_signal(barrier, inc=1, device_id={"req": neighbour}, device_id_type=MESH)

    @pl.when(me < n - 1)
    def _():
        pl.semaphore_signal(barrier, inc=1, device_id={"mp": me + 1}, device_id_type=MESH)

    @pl.when(me > 0)
    def _():
        pl.semaphore_signal(barrier, inc=1, device_id={"mp": me - 1}, device_id_type=MESH)

    gain = column_of(gain_ref[...].astype(jnp.float32))
    gath[0, me] = pack_pair(
        lat_ref[0, 0].astype(jnp.float32), lat_ref[1, 0].astype(jnp.float32), gain, packed
    ).astype(jnp.bfloat16)

    inner = (me > 0) & (me < n - 1)

    @pl.when(inner)
    def _():
        pl.semaphore_wait(barrier, 4)

    @pl.when(jnp.logical_not(inner))
    def _():
        pl.semaphore_wait(barrier, 3)

    half = rows // 2

    def piece(j, src):
        if j < 2:
            return gath.at[0, src, pl.ds(half * j, half)]
        return gath.at[1, src] if j == 2 else last.at[src]

    def up_copy(j, src):
        return pltpu.make_async_remote_copy(
            src_ref=piece(j, src),
            dst_ref=piece(j, src),
            send_sem=up_send.at[j, src],
            recv_sem=ag_recv.at[j, src],
            device_id={"mp": me + 1},
            device_id_type=MESH,
        )

    def down_copy(j, src):
        return pltpu.make_async_remote_copy(
            src_ref=piece(j, src),
            dst_ref=piece(j, src),
            send_sem=down_send.at[j, src],
            recv_sem=ag_recv.at[j, src],
            device_id={"mp": me - 1},
            device_id_type=MESH,
        )

    def send_own(j):
        @pl.when(me < n - 1)
        def _():
            up_copy(j, me).start()

        @pl.when(me > 0)
        def _():
            down_copy(j, me).start()

    def relay(j, d):
        @pl.when(me - d >= 0)
        def _():
            down_copy(j, me - d).wait_recv()

            @pl.when(me < n - 1)
            def _():
                up_copy(j, me - d).start()

        @pl.when(me + d <= n - 1)
        def _():
            up_copy(j, me + d).wait_recv()

            @pl.when(me > 0)
            def _():
                down_copy(j, me + d).start()

    send_own(0)
    send_own(1)

    slots = lat_ref.shape[0]
    offset = lax.rem(lax.div(move_ref[0], slots) - pos + ring, ring)
    first_right = jnp.where(offset == 1, 1.0, 0.0).astype(jnp.float32)
    pairs = []
    for s in range(2):
        label = jnp.full((rows, 1), lax.rem(move_ref[s], slots), jnp.int32).astype(jnp.float32)
        pairs.append(
            pack_pair(
                cache_ref[s, 0].astype(jnp.float32),
                cache_ref[s, 1].astype(jnp.float32),
                label,
                packed,
            )
        )
    pick = jnp.full((rows, packed), first_right, jnp.float32) > 0.5
    mig_out[0] = jnp.where(pick, pairs[0], pairs[1]).astype(jnp.bfloat16)
    mig_out[1] = jnp.where(pick, pairs[1], pairs[0]).astype(jnp.bfloat16)
    moves = []
    for k, neighbour in enumerate((right, left)):
        copy = pltpu.make_async_remote_copy(
            src_ref=mig_out.at[k],
            dst_ref=mig_in.at[k],
            send_sem=mig_send.at[k],
            recv_sem=mig_recv.at[k],
            device_id={"req": neighbour},
            device_id_type=MESH,
        )
        copy.start()
        moves.append(copy)

    relay(0, 1)
    relay(1, 1)
    for copy in moves:
        copy.wait_recv()
    from_left = mig_in[0].astype(jnp.float32)
    from_right = mig_in[1].astype(jnp.float32)
    to_second = jnp.broadcast_to(from_left[:, 2 * pixels : 2 * pixels + 1], (rows, packed)) > 0.5
    slot_0 = jnp.where(to_second, from_right, from_left)
    slot_1 = jnp.where(to_second, from_left, from_right)
    spill = packed - 2 * pixels
    turned = pltpu.roll(slot_1, packed - spill, axis=1)
    spare = lax.broadcasted_iota(jnp.int32, (rows, packed), 1) >= 2 * pixels
    gath[1, me] = jnp.where(spare, turned, slot_0).astype(jnp.bfloat16)
    last[me] = turned[:, : packed - 128].astype(jnp.bfloat16)
    send_own(2)
    send_own(3)
    for d in range(2, n):
        relay(0, d)
        relay(1, d)

    own = pl.multiple_of(me * rows, rows)
    values = gath[0].reshape(channels, packed).astype(jnp.float32)
    gains = values[:, 2 * pixels : 2 * pixels + 1]
    squares = jnp.sum(values * values, axis=0, keepdims=True)
    scaled = values * lax.rsqrt(squares / channels + 1e-06) * gains
    hidden = (scaled / (1.0 + jnp.exp(-scaled))).astype(jnp.bfloat16)
    stack[0, pl.ds(2 * channels, channels)] = hidden[:, :wide]
    stack[1, pl.ds(2 * channels, channels)] = second_half(hidden, pixels, wide)
    for copy in w_copies:
        copy.wait()
    taps = 9 * rows
    for s in range(2):
        new_ref[s, 1] = stack[s, pl.ds(2 * channels + own, rows), :pixels]
        acc[s] = jnp.dot(
            wcat[:, :, 2 * channels :].reshape(taps, channels),
            stack[s, pl.ds(2 * channels, channels)],
            preferred_element_type=jnp.float32,
        )

    def unpack(s, src):
        pair = gath[1, src]
        if s == 1:
            rest = last[src].astype(jnp.float32)
            head = pair[:, packed - 128 :].astype(jnp.float32)
            pair = jnp.concatenate([rest, head], axis=1)
            pair = pltpu.roll(pair, spill, axis=1).astype(jnp.bfloat16)
        at = pl.multiple_of(src * rows, rows)
        stack[s, pl.ds(at, rows)] = pair[:, :wide]
        stack[s, pl.ds(channels + at, rows)] = second_half(pair, pixels, wide)

    def unpack_arrived(s, d):
        @pl.when(me - d >= 0)
        def _():
            unpack(s, me - d)

        @pl.when(me + d <= n - 1)
        def _():
            unpack(s, me + d)

    unpack(0, me)
    unpack(1, me)
    for d in range(1, n - 1):
        relay(2, d)
        relay(3, d)
        unpack_arrived(0, d)
        unpack_arrived(1, d)

    lane = lax.broadcasted_iota(jnp.int32, (1, wide), 1)
    column = lax.rem(lane, row_width)
    bias = column_of(bias_ref[...])
    for s in range(2):
        relay(2 + s, n - 1)
        unpack_arrived(s, n - 1)
        new_ref[s, 0] = stack[s, pl.ds(channels + own, rows), :pixels]
        acc[s] += jnp.dot(
            wcat[:, :, : 2 * channels].reshape(taps, 2 * channels),
            stack[s, : 2 * channels],
            preferred_element_type=jnp.float32,
        )
        total = jnp.zeros((rows, wide), jnp.float32)
        for kx in range(3):
            part = acc[s, pl.ds((3 + kx) * rows, rows)]
            above = pltpu.roll(acc[s, pl.ds(kx * rows, rows)], row_width, axis=1)
            part = part + jnp.where(lane >= row_width, above, 0.0)
            below = pltpu.roll(acc[s, pl.ds((6 + kx) * rows, rows)], wide - row_width, axis=1)
            part = part + jnp.where(lane < pixels - row_width, below, 0.0)
            if kx == 0:
                part = jnp.where(column >= 1, pltpu.roll(part, 1, axis=1), 0.0)
            if kx == 2:
                part = jnp.where(column < row_width - 1, pltpu.roll(part, wide - 1, axis=1), 0.0)
            total = total + part
        result = lat_ref[s, 0].astype(jnp.float32) + (total + bias)[:, :pixels]
        live = jnp.full((rows, pixels), counts_ref[0], jnp.int32) > s
        dec_ref[s, 0] = jnp.where(live, result, 0.0).astype(jnp.bfloat16)

    for copy in moves:
        copy.wait_send()
    for j in range(4):
        for src in range(n):
            @pl.when((me < n - 1) & (src <= me))
            def _():
                up_copy(j, src).wait_send()

            @pl.when((me > 0) & (src >= me))
            def _():
                down_copy(j, src).wait_send()


def place_kernel(dec_ref, new_ref, dec_out, new_out):
    dec_out[...] = dec_ref[...]
    new_out[...] = new_ref[...]


def shards_kernel(latents, prior_frame_cache, move_to, counts, norm_gain, conv_weight, conv_bias):
    n, ring = lax.axis_size("mp"), lax.axis_size("req")
    rows, pixels = latents.shape[2], latents.shape[3]
    channels = n * rows
    packed, wide = lane_pad(2 * pixels + 1), lane_pad(pixels)
    vmem = pl.BlockSpec(memory_space=pltpu.VMEM)
    smem = pl.BlockSpec(memory_space=pltpu.SMEM)
    results = pl.pallas_call(
        functools.partial(block_kernel, n, ring, LATENT_COLUMNS),
        out_shape=(
            pltpu.VMEM(latents.shape, jnp.bfloat16),
            pltpu.VMEM(prior_frame_cache.shape, jnp.bfloat16),
        ),
        in_specs=[smem, smem, vmem, vmem, vmem, vmem, pl.BlockSpec(memory_space=pltpu.HBM)],
        out_specs=(vmem, vmem),
        scratch_shapes=[
            pltpu.VMEM((9, rows, 3 * channels), jnp.bfloat16),
            pltpu.VMEM((2, n, rows, packed), jnp.bfloat16),
            pltpu.VMEM((n, rows, packed - 128), jnp.bfloat16),
            pltpu.VMEM((2, rows, packed), jnp.bfloat16),
            pltpu.VMEM((2, rows, packed), jnp.bfloat16),
            pltpu.VMEM((2, 3 * channels, wide), jnp.bfloat16),
            pltpu.VMEM((2, 9 * rows, wide), jnp.float32),
            pltpu.SemaphoreType.DMA((3,)),
            pltpu.SemaphoreType.DMA((2,)),
            pltpu.SemaphoreType.DMA((2,)),
            pltpu.SemaphoreType.DMA((4, n)),
            pltpu.SemaphoreType.DMA((4, n)),
            pltpu.SemaphoreType.DMA((4, n)),
        ],
        compiler_params=pltpu.CompilerParams(
            collective_id=0, has_side_effects=True, vmem_limit_bytes=63 << 20
        ),
    )(
        move_to,
        counts,
        latents,
        prior_frame_cache,
        norm_gain.reshape(1, rows),
        conv_bias.reshape(1, rows),
        conv_weight,
    )
    return pl.pallas_call(
        place_kernel,
        out_shape=tuple(jax.ShapeDtypeStruct(r.shape, r.dtype) for r in results),
        in_specs=[vmem, vmem],
        out_specs=(vmem, vmem),
        compiler_params=pltpu.CompilerParams(vmem_limit_bytes=8 << 20),
    )(*results)


def shards(latents, *rest):
    fits = (
        latents.shape[0] == 2
        and latents.shape[1] == 1
        and latents.shape[2] % 32 == 0
        and latents.shape[3] % 128 == 32
        and lax.axis_size("req") > 2
        and lax.axis_size("mp") > 1
        and lax.axis_size("mp") * latents.shape[2] % 128 == 0
    )
    return (shards_kernel if fits else shards_plain)(latents, *rest)


def solution(mesh):
    in_specs = (
        P("req", None, "mp", None),
        P("req", None, "mp", None),
        P("req"),
        P("req"),
        P("mp"),
        P(None, "mp", None),
        P("mp"),
    )
    out_specs = (P("req", None, "mp", None), P("req", None, "mp", None))
    return jax.shard_map(shards, mesh=mesh, in_specs=in_specs, out_specs=out_specs, check_vma=False)
```

```python
import functools

import jax
import jax.numpy as jnp
from jax import lax
from jax.experimental import pallas as pl
from jax.experimental.pallas import tpu as pltpu
from jax.sharding import PartitionSpec as P

SECTION_CHANNELS = 384
LATENT_COLUMNS = 104


def shifted_2(block, axis, distance):
    devices = range(lax.axis_size(axis))
    route = [((i - distance) % len(devices), i) for i in devices]
    return lax.ppermute(block, axis, route)


def apply_taps(running, shard_in, weights, row_width):
    frames = shard_in.shape[1] - 2
    pixels = shard_in.shape[3]
    padded = jnp.pad(shard_in, ((0, 0), (0, 0), (0, 0), (row_width + 1, row_width + 1)))
    column = jnp.arange(pixels + 2 * row_width) % row_width
    for step_x in range(3):
        inside = ((column + step_x - 1 >= 0) & (column + step_x - 1 < row_width)).astype(
            shard_in.dtype
        )
        shifted = padded[:, :, :, step_x : step_x + pixels + 2 * row_width] * inside
        for step_y in range(3):
            window = shifted[:, :, :, step_y * row_width : step_y * row_width + pixels]
            for step_t in range(3):
                running = running + jnp.einsum(
                    "oc,stcp->stop",
                    weights[step_t * 9 + step_y * 3 + step_x],
                    window[:, step_t : step_t + frames],
                    preferred_element_type=jnp.float32,
                )
    return running


def pack_slots(prior_frame_cache, chosen, target, capacity):
    ranking = jnp.cumsum(chosen.astype(jnp.int32)) - 1
    picker = (chosen[None, :] & (ranking[None, :] == jnp.arange(capacity)[:, None])).astype(
        jnp.bfloat16
    )
    blocks = jnp.einsum(
        "cs,sfkp->cfkp", picker, prior_frame_cache, preferred_element_type=jnp.float32
    ).astype(jnp.bfloat16)
    labels = (jnp.dot(picker.astype(jnp.float32), (target + 1).astype(jnp.float32)) - 1.0).astype(
        jnp.bfloat16
    )
    return (blocks, labels)


def migrate(prior_frame_cache, move_to):
    slot_count = prior_frame_cache.shape[0]
    member_slots = lax.axis_size("req")
    position = lax.axis_index("req")
    capacity = slot_count // 2
    device = move_to // slot_count
    target = move_to % slot_count
    offset = (device - position) % member_slots
    goes_right = offset == 1
    goes_left = offset == member_slots - 1
    stays_put = offset == 0
    blocks_right, labels_right = pack_slots(prior_frame_cache, goes_right, target, capacity)
    blocks_left, labels_left = pack_slots(prior_frame_cache, goes_left, target, capacity)
    from_left = shifted_2((blocks_right, labels_right), "req", 1)
    from_right = shifted_2((blocks_left, labels_left), "req", -1)
    sources = jnp.concatenate([prior_frame_cache, from_left[0], from_right[0]], axis=0)
    own_labels = jnp.where(stays_put, target, -1).astype(jnp.float32)
    labels = jnp.concatenate(
        [own_labels, from_left[1].astype(jnp.float32), from_right[1].astype(jnp.float32)]
    )
    placing = (labels[None, :] == jnp.arange(slot_count, dtype=jnp.float32)[:, None]).astype(
        jnp.bfloat16
    )
    return jnp.einsum("ns,sfkp->nfkp", placing, sources, preferred_element_type=jnp.float32).astype(
        jnp.bfloat16
    )


def normalize(values, squares, gains):
    scaled = (
        values.astype(jnp.float32)
        * lax.rsqrt(squares / SECTION_CHANNELS + 1e-06)
        * gains.astype(jnp.float32)[:, None]
    )
    return jax.nn.silu(scaled).astype(jnp.bfloat16)


def shards_plain(latents, prior_frame_cache, move_to, counts, norm_gain, conv_weight, conv_bias):
    moved = migrate(prior_frame_cache, move_to)
    slot_count = latents.shape[0]
    frames = latents.shape[1]
    live = (jnp.arange(slot_count) < counts[0])[:, None, None, None]
    start_zero = jnp.zeros(
        (slot_count, frames, conv_weight.shape[1], latents.shape[3]), jnp.float32
    )
    values = latents.astype(jnp.float32)
    partial_squares = jnp.sum(values * values, axis=2, keepdims=True)
    squares = lax.psum(partial_squares, "mp")
    hidden = normalize(latents, squares, norm_gain)
    extended = jnp.concatenate([moved, hidden], axis=1)
    conv_sum = apply_taps(
        start_zero, lax.all_gather(extended, "mp", axis=2, tiled=True), conv_weight, LATENT_COLUMNS
    )
    total = latents.astype(jnp.float32) + conv_sum + conv_bias[:, None]
    decoded = jnp.where(live, total, jnp.zeros_like(total)).astype(jnp.bfloat16)
    new_cache = extended[:, frames:]
    return (decoded, new_cache)


MESH = pl.DeviceIdType.MESH


def lane_pad(n):
    return (n + 127) // 128 * 128


def column_of(row):
    n = row.shape[1]
    square = lax.broadcasted_iota(jnp.int32, (n, n), 0) == lax.broadcasted_iota(
        jnp.int32, (n, n), 1
    )
    return jnp.sum(jnp.where(square, jnp.broadcast_to(row, (n, n)), 0.0), axis=1, keepdims=True)


def pack_pair(first, second, extra, packed):
    rows, pixels = first.shape
    tail = jnp.broadcast_to(extra, (rows, packed - 2 * pixels))
    return jnp.concatenate([first, second, tail], axis=1)


def second_half(pair, pixels, wide):
    start = pixels // 128 * 128
    part = pair[:, start : start + wide].astype(jnp.float32)
    return pltpu.roll(part, wide - pixels % 128, axis=1).astype(jnp.bfloat16)


def block_kernel(
    n,
    ring,
    row_width,
    move_ref,
    counts_ref,
    lat_ref,
    cache_ref,
    gain_ref,
    bias_ref,
    w_ref,
    dec_ref,
    new_ref,
    wcat,
    gath,
    last,
    mig_out,
    mig_in,
    stack,
    acc,
    w_sem,
    mig_send,
    mig_recv,
    up_send,
    down_send,
    ag_recv,
):
    me = lax.axis_index("mp")
    pos = lax.axis_index("req")
    rows, pixels = lat_ref.shape[2], lat_ref.shape[3]
    packed = gath.shape[3]
    wide = stack.shape[2]
    channels = n * rows
    right, left = lax.rem(pos + 1, ring), lax.rem(pos + ring - 1, ring)

    w_copies = []
    for kt in range(3):
        copy = pltpu.make_async_copy(
            w_ref.at[pl.ds(9 * kt, 9)],
            wcat.at[:, :, pl.ds(channels * kt, channels)],
            w_sem.at[kt],
        )
        copy.start()
        w_copies.append(copy)

    barrier = pltpu.get_barrier_semaphore()
    for neighbour in (right, left):
        pl.semaphore_signal(barrier, inc=1, device_id={"req": neighbour}, device_id_type=MESH)

    @pl.when(me < n - 1)
    def _():
        pl.semaphore_signal(barrier, inc=1, device_id={"mp": me + 1}, device_id_type=MESH)

    @pl.when(me > 0)
    def _():
        pl.semaphore_signal(barrier, inc=1, device_id={"mp": me - 1}, device_id_type=MESH)

    gain = column_of(gain_ref[...].astype(jnp.float32))
    gath[0, me] = pack_pair(
        lat_ref[0, 0].astype(jnp.float32), lat_ref[1, 0].astype(jnp.float32), gain, packed
    ).astype(jnp.bfloat16)

    inner = (me > 0) & (me < n - 1)

    @pl.when(inner)
    def _():
        pl.semaphore_wait(barrier, 4)

    @pl.when(jnp.logical_not(inner))
    def _():
        pl.semaphore_wait(barrier, 3)

    half = rows // 2

    def piece(j, src):
        if j < 2:
            return gath.at[0, src, pl.ds(half * j, half)]
        return gath.at[1, src] if j == 2 else last.at[src]

    def up_copy(j, src):
        return pltpu.make_async_remote_copy(
            src_ref=piece(j, src),
            dst_ref=piece(j, src),
            send_sem=up_send.at[j, src],
            recv_sem=ag_recv.at[j, src],
            device_id={"mp": me + 1},
            device_id_type=MESH,
        )

    def down_copy(j, src):
        return pltpu.make_async_remote_copy(
            src_ref=piece(j, src),
            dst_ref=piece(j, src),
            send_sem=down_send.at[j, src],
            recv_sem=ag_recv.at[j, src],
            device_id={"mp": me - 1},
            device_id_type=MESH,
        )

    def send_own(j):
        @pl.when(me < n - 1)
        def _():
            up_copy(j, me).start()

        @pl.when(me > 0)
        def _():
            down_copy(j, me).start()

    def relay_up(j, d):
        @pl.when(me - d >= 0)
        def _():
            down_copy(j, me - d).wait_recv()

            @pl.when(me < n - 1)
            def _():
                up_copy(j, me - d).start()

    def relay_down(j, d):
        @pl.when(me + d <= n - 1)
        def _():
            up_copy(j, me + d).wait_recv()

            @pl.when(me > 0)
            def _():
                down_copy(j, me + d).start()

    def relay(j, d):
        @pl.when(2 * me >= n)
        def _():
            relay_up(j, d)
            relay_down(j, d)

        @pl.when(2 * me < n)
        def _():
            relay_down(j, d)
            relay_up(j, d)

    send_own(0)
    send_own(1)

    slots = lat_ref.shape[0]
    offset = lax.rem(lax.div(move_ref[0], slots) - pos + ring, ring)
    first_right = jnp.where(offset == 1, 1.0, 0.0).astype(jnp.float32)
    pairs = []
    for s in range(2):
        label = jnp.full((rows, 1), lax.rem(move_ref[s], slots), jnp.int32).astype(jnp.float32)
        pairs.append(
            pack_pair(
                cache_ref[s, 0].astype(jnp.float32),
                cache_ref[s, 1].astype(jnp.float32),
                label,
                packed,
            )
        )
    pick = jnp.full((rows, packed), first_right, jnp.float32) > 0.5
    mig_out[0] = jnp.where(pick, pairs[0], pairs[1]).astype(jnp.bfloat16)
    mig_out[1] = jnp.where(pick, pairs[1], pairs[0]).astype(jnp.bfloat16)
    moves = []
    for k, neighbour in enumerate((right, left)):
        copy = pltpu.make_async_remote_copy(
            src_ref=mig_out.at[k],
            dst_ref=mig_in.at[k],
            send_sem=mig_send.at[k],
            recv_sem=mig_recv.at[k],
            device_id={"req": neighbour},
            device_id_type=MESH,
        )
        copy.start()
        moves.append(copy)

    relay(0, 1)
    relay(1, 1)
    for copy in moves:
        copy.wait_recv()
    from_left = mig_in[0].astype(jnp.float32)
    from_right = mig_in[1].astype(jnp.float32)
    to_second = jnp.broadcast_to(from_left[:, 2 * pixels : 2 * pixels + 1], (rows, packed)) > 0.5
    slot_0 = jnp.where(to_second, from_right, from_left)
    slot_1 = jnp.where(to_second, from_left, from_right)
    spill = packed - 2 * pixels
    turned = pltpu.roll(slot_1, packed - spill, axis=1)
    spare = lax.broadcasted_iota(jnp.int32, (rows, packed), 1) >= 2 * pixels
    gath[1, me] = jnp.where(spare, turned, slot_0).astype(jnp.bfloat16)
    last[me] = turned[:, : packed - 128].astype(jnp.bfloat16)
    send_own(2)
    send_own(3)
    for d in range(2, n):
        relay(0, d)
        relay(1, d)

    own = pl.multiple_of(me * rows, rows)
    values = gath[0].reshape(channels, packed).astype(jnp.float32)
    gains = values[:, 2 * pixels : 2 * pixels + 1]
    squares = jnp.sum(values * values, axis=0, keepdims=True)
    scaled = values * lax.rsqrt(squares / channels + 1e-06) * gains
    hidden = (scaled / (1.0 + jnp.exp(-scaled))).astype(jnp.bfloat16)
    stack[0, pl.ds(2 * channels, channels)] = hidden[:, :wide]
    stack[1, pl.ds(2 * channels, channels)] = second_half(hidden, pixels, wide)
    for copy in w_copies:
        copy.wait()
    taps = 9 * rows
    for s in range(2):
        new_ref[s, 1] = stack[s, pl.ds(2 * channels + own, rows), :pixels]
        acc[s] = jnp.dot(
            wcat[:, :, 2 * channels :].reshape(taps, channels),
            stack[s, pl.ds(2 * channels, channels)],
            preferred_element_type=jnp.float32,
        )

    def unpack(s, src):
        pair = gath[1, src]
        if s == 1:
            rest = last[src].astype(jnp.float32)
            head = pair[:, packed - 128 :].astype(jnp.float32)
            pair = jnp.concatenate([rest, head], axis=1)
            pair = pltpu.roll(pair, spill, axis=1).astype(jnp.bfloat16)
        at = pl.multiple_of(src * rows, rows)
        stack[s, pl.ds(at, rows)] = pair[:, :wide]
        stack[s, pl.ds(channels + at, rows)] = second_half(pair, pixels, wide)

    def unpack_arrived(s, d):
        @pl.when(me - d >= 0)
        def _():
            unpack(s, me - d)

        @pl.when(me + d <= n - 1)
        def _():
            unpack(s, me + d)

    unpack(0, me)
    unpack(1, me)
    for d in range(1, n - 1):
        relay(2, d)
        relay(3, d)
        unpack_arrived(0, d)
        unpack_arrived(1, d)

    lane = lax.broadcasted_iota(jnp.int32, (1, wide), 1)
    column = lax.rem(lane, row_width)
    bias = column_of(bias_ref[...])
    for s in range(2):
        relay(2 + s, n - 1)
        unpack_arrived(s, n - 1)
        new_ref[s, 0] = stack[s, pl.ds(channels + own, rows), :pixels]
        acc[s] += jnp.dot(
            wcat[:, :, : 2 * channels].reshape(taps, 2 * channels),
            stack[s, : 2 * channels],
            preferred_element_type=jnp.float32,
        )
        total = jnp.zeros((rows, wide), jnp.float32)
        for kx in range(3):
            part = acc[s, pl.ds((3 + kx) * rows, rows)]
            above = pltpu.roll(acc[s, pl.ds(kx * rows, rows)], row_width, axis=1)
            part = part + jnp.where(lane >= row_width, above, 0.0)
            below = pltpu.roll(acc[s, pl.ds((6 + kx) * rows, rows)], wide - row_width, axis=1)
            part = part + jnp.where(lane < pixels - row_width, below, 0.0)
            if kx == 0:
                part = jnp.where(column >= 1, pltpu.roll(part, 1, axis=1), 0.0)
            if kx == 2:
                part = jnp.where(column < row_width - 1, pltpu.roll(part, wide - 1, axis=1), 0.0)
            total = total + part
        result = lat_ref[s, 0].astype(jnp.float32) + (total + bias)[:, :pixels]
        live = jnp.full((rows, pixels), counts_ref[0], jnp.int32) > s
        dec_ref[s, 0] = jnp.where(live, result, 0.0).astype(jnp.bfloat16)

    for copy in moves:
        copy.wait_send()
    for j in range(4):
        for src in range(n):
            @pl.when((me < n - 1) & (src <= me))
            def _():
                up_copy(j, src).wait_send()

            @pl.when((me > 0) & (src >= me))
            def _():
                down_copy(j, src).wait_send()


def place_kernel(dec_ref, new_ref, dec_out, new_out):
    dec_out[...] = dec_ref[...]
    new_out[...] = new_ref[...]


def shards_kernel(latents, prior_frame_cache, move_to, counts, norm_gain, conv_weight, conv_bias):
    n, ring = lax.axis_size("mp"), lax.axis_size("req")
    rows, pixels = latents.shape[2], latents.shape[3]
    channels = n * rows
    packed, wide = lane_pad(2 * pixels + 1), lane_pad(pixels)
    vmem = pl.BlockSpec(memory_space=pltpu.VMEM)
    smem = pl.BlockSpec(memory_space=pltpu.SMEM)
    results = pl.pallas_call(
        functools.partial(block_kernel, n, ring, LATENT_COLUMNS),
        out_shape=(
            pltpu.VMEM(latents.shape, jnp.bfloat16),
            pltpu.VMEM(prior_frame_cache.shape, jnp.bfloat16),
        ),
        in_specs=[smem, smem, vmem, vmem, vmem, vmem, pl.BlockSpec(memory_space=pltpu.HBM)],
        out_specs=(vmem, vmem),
        scratch_shapes=[
            pltpu.VMEM((9, rows, 3 * channels), jnp.bfloat16),
            pltpu.VMEM((2, n, rows, packed), jnp.bfloat16),
            pltpu.VMEM((n, rows, packed - 128), jnp.bfloat16),
            pltpu.VMEM((2, rows, packed), jnp.bfloat16),
            pltpu.VMEM((2, rows, packed), jnp.bfloat16),
            pltpu.VMEM((2, 3 * channels, wide), jnp.bfloat16),
            pltpu.VMEM((2, 9 * rows, wide), jnp.float32),
            pltpu.SemaphoreType.DMA((3,)),
            pltpu.SemaphoreType.DMA((2,)),
            pltpu.SemaphoreType.DMA((2,)),
            pltpu.SemaphoreType.DMA((4, n)),
            pltpu.SemaphoreType.DMA((4, n)),
            pltpu.SemaphoreType.DMA((4, n)),
        ],
        compiler_params=pltpu.CompilerParams(
            collective_id=0, has_side_effects=True, vmem_limit_bytes=63 << 20
        ),
    )(
        move_to,
        counts,
        latents,
        prior_frame_cache,
        norm_gain.reshape(1, rows),
        conv_bias.reshape(1, rows),
        conv_weight,
    )
    return pl.pallas_call(
        place_kernel,
        out_shape=tuple(jax.ShapeDtypeStruct(r.shape, r.dtype) for r in results),
        in_specs=[vmem, vmem],
        out_specs=(vmem, vmem),
        compiler_params=pltpu.CompilerParams(vmem_limit_bytes=8 << 20),
    )(*results)


def shards(latents, *rest):
    fits = (
        latents.shape[0] == 2
        and latents.shape[1] == 1
        and latents.shape[2] % 32 == 0
        and latents.shape[3] % 128 == 32
        and lax.axis_size("req") > 2
        and lax.axis_size("mp") > 1
        and lax.axis_size("mp") * latents.shape[2] % 128 == 0
    )
    return (shards_kernel if fits else shards_plain)(latents, *rest)


def solution(mesh):
    in_specs = (
        P("req", None, "mp", None),
        P("req", None, "mp", None),
        P("req"),
        P("req"),
        P("mp"),
        P(None, "mp", None),
        P("mp"),
    )
    out_specs = (P("req", None, "mp", None), P("req", None, "mp", None))
    return jax.shard_map(shards, mesh=mesh, in_specs=in_specs, out_specs=out_specs, check_vma=False)
```
